32 devices in a mesh: dp: 4 (over x, core), context: 8 (over z, y).
Axes of the slice: x: 2, y: 2, z: 4, core: 2. Of those that a mesh axis runs over, the one named last changes fastest.
Arguments:
- signal: bfloat16 [8192, 2048], P('context', 'dp'), may hold values from -6 to 6
- gating: bfloat16 [8192, 2048], P('context', 'dp'), may hold values from -6 to 6
- writer: bfloat16 [8192, 128], P('context'), may hold values from -2 to 2
- reader: bfloat16 [8192, 128], P('context'), may hold values from -2 to 2
- step_raw: float32 [8192, 32], P('context', 'dp'), may hold values from -7 to -1
- decay_log: float32 [32], P('dp'), may hold values from -12 to 1
- skip_gain: float32 [32], P('dp'), may hold values from 0.5 to 2
- norm_gain: float32 [2048], P('dp'), may hold values from 0.25 to 1.75
- cotangent: bfloat16 [8192, 2048], P('context', 'dp'), may hold values from -6 to 6
Outputs:
- grad_signal: bfloat16 [8192, 2048], P('context', 'dp')
- grad_gating: bfloat16 [8192, 2048], P('context', 'dp')
- grad_bc: float32 [8192, 256], P('context', 'dp')
- grad_step: float32 [8192, 32], P('context', 'dp')
The draws below stay inside these ranges and needn't reach their ends.
All inputs are finite; a program needn't handle non-finite values.
Results may differ from the reference program's by a relative error of at most 0.0011.
Values sent between devices are 32-bit elements; how exact they have to be, the bound alone decides.
No kernel may reach another device: no remote copies, remote signals or barrier semaphores. Data moves between devices by JAX's collectives and lax.ppermute only.
A program may use at most 64 MiB of HBM per device.

```python
from functools import partial
import jax
import jax.numpy as jnp
from jax import lax

HEADS = 32
HEAD_DIM = 64
STATE = 128
SPAN = 256
TOKENS = 8192


def draw_decay_log(key, part):
    subkeys = jax.random.split(jax.random.fold_in(key, 17), 2)
    ordering = jax.random.permutation(subkeys[0], HEADS)
    keeping = HEADS // 2
    slowness = ordering < keeping
    spreads = jax.random.uniform(subkeys[1], (HEADS,), jnp.float32)
    slow_log = -jnp.log(TOKENS * 0.03) - 1.5 + 2.0 * spreads
    fast_log = jnp.log(1.25) - 1.4 + 2.1 * spreads
    return jnp.where(slowness, slow_log, fast_log).astype(jnp.float32)


def draw_step_raw(key, part):
    fluctuation = jax.random.normal(jax.random.fold_in(key, 23), (TOKENS, HEADS), jnp.float32)
    return (-4.0 + jnp.clip(fluctuation, -3.0, 3.0)).astype(jnp.float32)


def levels(stream_key, dims, shards, low, high):
    loudness, own = 1.0, jax.random.fold_in(stream_key, 6)
    for dim, parts in shards:
        draws = jnp.exp(jax.random.uniform(jax.random.fold_in(own, dim), (parts,), jnp.float32, low / len(shards), high / len(shards)))
        loudness = loudness * jnp.repeat(draws, dims[dim] // parts).reshape([-1 if axis == dim else 1 for axis in range(len(dims))])
    return loudness


def gaussian(own_key, extent, scale, limit, shards=(), kind=jnp.bfloat16):
    values = jax.random.normal(own_key, extent, jnp.float32) * scale
    if len(shards) > 0:
        values = levels(own_key, extent, shards, -0.22, 0.18) * values
    return jnp.clip(values, min=-limit, max=limit).astype(kind)


def setup_inputs(seed: int = 0) -> dict:
    splits = jax.random.split(jax.random.key(seed), 10)
    return {
        "signal": gaussian(splits[0], (TOKENS, HEADS * HEAD_DIM), 1.0, 6.0, ((0, 8), (1, 4))),
        "gating": gaussian(splits[1], (TOKENS, HEADS * HEAD_DIM), 1.0, 6.0, ((0, 8), (1, 4))),
        "writer": gaussian(splits[2], (TOKENS, STATE), 0.3, 2.0, ((0, 8),)),
        "reader": gaussian(splits[3], (TOKENS, STATE), 0.3, 2.0, ((0, 8),)),
        "step_raw": draw_step_raw(jax.random.fold_in(splits[9], 71), 0),
        "decay_log": draw_decay_log(jax.random.fold_in(splits[9], 71), 0),
        "skip_gain": jnp.clip(0.5 + 1.5 * jax.random.uniform(splits[6], (HEADS,), jnp.float32) ** levels(splits[6], (HEADS,), ((0, 4),), -0.2, 0.2), 0.5, 2.0),
        "norm_gain": jnp.clip(1.0 + 0.15 * jax.random.normal(splits[7], (HEADS * HEAD_DIM,), jnp.float32), 0.25, 1.75),
        "cotangent": gaussian(splits[8], (TOKENS, HEADS * HEAD_DIM), 1.0, 6.0, ((0, 8), (1, 4))),
    }


highest = lax.Precision.HIGHEST
epsilon = 1e-05

def block_step(state, pieces, decay_rate, skip_gain):
    signal_block, writer_block, reader_block, raw_block = pieces
    step_size = jax.nn.softplus(raw_block)
    log_decay = step_size * decay_rate[None, :]
    running = jnp.cumsum(log_decay, axis=0)
    length = raw_block.shape[0]
    causal = jnp.arange(length)[:, None] >= jnp.arange(length)[None, :]
    log_gaps = running[:, None, :] - running[None, :, :]
    decays = jnp.exp(jnp.where(causal[:, :, None], log_gaps, -jnp.inf))
    scores = jnp.dot(reader_block, writer_block.T, precision=highest, preferred_element_type=jnp.float32)
    mixing = scores[:, :, None] * decays * step_size[None, :, :]
    within = jnp.einsum('tsh,shp->thp', mixing, signal_block, precision=highest)
    across = jnp.exp(running)[:, :, None] * jnp.einsum('tn,hpn->thp', reader_block, state, precision=highest)
    result = within + across + skip_gain[None, :, None] * signal_block
    weights = jnp.exp(running[-1][None, :] - running) * step_size
    new_state = jnp.exp(running[-1])[:, None, None] * state + jnp.einsum('sh,shp,sn->hpn', weights, signal_block, writer_block, precision=highest)
    return (new_state, result)

def recurrence(signal, writer, reader, step_raw, start_state, decay_rate, skip_gain):
    tokens, head_count = step_raw.shape
    blocks = tokens // SPAN
    pieces = (signal.reshape(blocks, SPAN, head_count, HEAD_DIM), writer.reshape(blocks, SPAN, -1), reader.reshape(blocks, SPAN, -1), step_raw.reshape(blocks, SPAN, head_count))
    advance = jax.checkpoint(partial(block_step, decay_rate=decay_rate, skip_gain=skip_gain))
    end_state, outputs = lax.scan(advance, start_state, pieces)
    return (outputs.reshape(tokens, head_count * HEAD_DIM), end_state)

def reference(signal, gating, writer, reader, step_raw, decay_log, skip_gain, norm_gain, cotangent):
    decay_rate = -jnp.exp(decay_log)

    def forward(signal_f, gating_f, writer_f, reader_f, raw_f):
        start_state = jnp.zeros((raw_f.shape[1], HEAD_DIM, writer_f.shape[1]), jnp.float32)
        output, end_state = recurrence(signal_f, writer_f, reader_f, raw_f, start_state, decay_rate, skip_gain)
        gated_output = output * jax.nn.silu(gating_f)
        scaling = lax.rsqrt(lax.optimization_barrier(jnp.mean(gated_output * gated_output, axis=1, keepdims=True)) + epsilon)
        return gated_output * scaling * norm_gain[None, :]
    primals = (signal.astype(jnp.float32), gating.astype(jnp.float32), writer.astype(jnp.float32), reader.astype(jnp.float32), step_raw)
    normed, pullback = jax.vjp(forward, *primals)
    grad_signal, grad_gating, grad_writer, grad_reader, grad_step = pullback(cotangent.astype(jnp.float32))
    return (grad_signal.astype(jnp.bfloat16), grad_gating.astype(jnp.bfloat16), jnp.concatenate([grad_writer, grad_reader], axis=1), grad_step)
```

```python
from functools import partial

import jax
import jax.numpy as jnp
from jax import lax
from jax.experimental import pallas as pl
from jax.experimental.pallas import tpu as pltpu
from jax.sharding import PartitionSpec as P

HEAD_DIM = 64
BLOCK = 128
EPSILON = 1e-05
F32 = jnp.float32
BF16 = jnp.bfloat16
NEGATIVE = -1e30
DT, RUN, ALL, LATE, SIG, LAST = range(6)


def dot(a, b):
    return lax.dot_general(a, b, (((1,), (0,)), ((), ())), preferred_element_type=F32)


def dot_nt(a, b):
    return lax.dot_general(a, b, (((1,), (1,)), ((), ())), preferred_element_type=F32)


def split2(x):
    high = x.astype(BF16)
    return high, (x - high.astype(F32)).astype(BF16)


def split3(x):
    high = x.astype(BF16)
    rest = x - high.astype(F32)
    middle = rest.astype(BF16)
    return high, middle, (rest - middle.astype(F32)).astype(BF16)


def iota(shape, axis):
    return lax.broadcasted_iota(jnp.int32, shape, axis)


def lanes(*parts):
    return jnp.concatenate(parts, axis=1)


def rows(*parts):
    return jnp.concatenate(parts, axis=0)


def transposed(x):
    return x.astype(F32).T.astype(BF16)


def padded(head_count):
    return -(-head_count // 8) * 8


def columns(values):
    pieces = [p.astype(F32) for v in values for p in split3(v)]
    used = sum(p.shape[0] for p in pieces)
    return rows(*pieces, jnp.zeros((BLOCK - used, BLOCK), F32)).T.astype(BF16)


def plain_columns(*values):
    used = sum(v.shape[0] for v in values)
    return rows(*values, jnp.zeros((BLOCK - used, BLOCK), F32)).T


def spread(place, group, width):
    row = iota((BLOCK, width), 0) - 3 * group * place
    head = iota((BLOCK, width), 1) // HEAD_DIM
    hit = (row == head) | (row == head + group) | (row == head + 2 * group)
    return hit.astype(F32).astype(BF16)


def gather_heads(group, width, copies):
    one = (iota((group, width), 0) == iota((group, width), 1) // HEAD_DIM).astype(F32).astype(BF16)
    return lanes(*([one] * copies))


def head_scalars(ref, shape, axis, per):
    place = iota(shape, axis) // per
    out = jnp.zeros(shape, F32)
    for h in range(ref.shape[0]):
        out = jnp.where(place == h, ref[h], out)
    return out


def part(table, which, group):
    return table[which * group : (which + 1) * group, :]


def halves(x, parity):
    half = x.shape[1] // 2
    first, second = x[:, :half], x[:, half:]
    return jnp.where(parity == 0, first, second), jnp.where(parity == 0, second, first)


def joined(mine, other, parity, count):
    m, o = mine[:count, :], other[:count, :]
    return lanes(jnp.where(parity == 0, m, o), jnp.where(parity == 0, o, m))


def lane_totals(total, group, width):
    return dot(columns([total]), spread(0, group, width))


def causal_mask(transpose):
    a, b = iota((BLOCK, BLOCK), 0), iota((BLOCK, BLOCK), 1)
    return b >= a if transpose else a >= b


def ends_kernel(decay_ref, raw_ref, signal_ref, writer_ref, table_ref, mine_ref, theirs_ref):
    tokens, head_count = raw_ref.shape
    width = signal_ref.shape[1]
    group = padded(head_count)
    parity = lax.axis_index("context") % 2
    eye = (iota((group, head_count), 0) == iota((group, head_count), 1)).astype(F32).astype(BF16)
    raw = sum(dot_nt(eye, p) for p in split3(raw_ref[...]))
    step = jnp.maximum(raw, 0.0) + jnp.log1p(jnp.exp(-jnp.abs(raw)))
    rate = -jnp.exp(head_scalars(decay_ref, (group, BLOCK), 0, 1))
    upper = causal_mask(True).astype(F32).astype(BF16)
    blocks = tokens // BLOCK
    offset = jnp.zeros((group, 1), F32)
    running, overall, steps = [], [], []
    for c in range(blocks):
        step_c = step[:, c * BLOCK : (c + 1) * BLOCK]
        run = sum(dot(p, upper) for p in split3(step_c * rate))
        running.append(run)
        steps.append(step_c)
        overall.append(run + offset)
        offset = offset + run[:, BLOCK - 1 : BLOCK]
    state = jnp.zeros((writer_ref.shape[1], width), F32)
    weight_spread = spread(0, group, width)
    for c in range(blocks):
        cut = slice(c * BLOCK, (c + 1) * BLOCK)
        raw_c = raw[:, cut]
        last = jnp.exp(offset - overall[c]) * steps[c]
        table_ref[:, cut] = rows(
            steps[c],
            running[c],
            overall[c],
            running[c] - jnp.log(steps[c]),
            1.0 / (1.0 + jnp.exp(-raw_c)),
            last,
        )
        weights = dot(columns([last]), weight_spread)
        high, low = split2(weights * signal_ref[cut, :].astype(F32))
        turned = transposed(writer_ref[cut, :])
        state = state + dot(lanes(turned, turned), rows(high, low))
    totals = lane_totals(jnp.broadcast_to(offset, (group, BLOCK)), group, width)[:8]
    mine, theirs = halves(rows(state, totals), parity)
    mine_ref[...] = mine
    theirs_ref[...] = theirs


def forward_kernel(
    skip_ref, table_ref, signal_ref, writer_ref, reader_ref, output_ref, states_ref, state
):
    width = signal_ref.shape[1]
    head_count = width // HEAD_DIM
    group = padded(head_count)

    @pl.when(pl.program_id(0) == 0)
    def _():
        state[...] = jnp.zeros_like(state)

    table = table_ref[...]
    run, late, step = part(table, RUN, group), part(table, LATE, group), part(table, DT, group)
    total = run[:, BLOCK - 1 : BLOCK]
    signal, writer, reader = signal_ref[...], writer_ref[...], reader_ref[...]
    signal_f = signal.astype(F32)
    cols = columns([jnp.exp(run), jnp.exp(total - run) * step])
    opening = dot(cols, spread(0, group, width))
    weights = dot(cols, spread(1, group, width))
    shrink = lane_totals(jnp.broadcast_to(total, (group, BLOCK)), group, width)
    state_now = state[...]
    states_ref[0] = state_now
    high, low = split2(state_now)
    across = opening * dot(lanes(reader, reader), rows(high, low))
    skip = head_scalars(skip_ref, (1, width), 1, HEAD_DIM)
    base = across + skip * signal_f
    scores = dot_nt(reader, writer)
    allowed = causal_mask(False)
    run_cols = plain_columns(run)
    low_lane = iota((BLOCK, BLOCK), 1) < HEAD_DIM
    for j in range(head_count // 2):
        cut = slice(j * BLOCK, (j + 1) * BLOCK)
        pair = signal_f[:, cut]
        left, right = [], []
        for k in range(2):
            h = 2 * j + k
            gap = run_cols[:, h : h + 1] - late[h : h + 1, :]
            mixing = scores * jnp.exp(jnp.where(allowed, gap, NEGATIVE))
            left += list(split2(mixing))
            own = jnp.where(low_lane == (k == 0), pair, 0.0).astype(BF16)
            right += [own, own]
        output_ref[:, cut] = base[:, cut] + dot(lanes(*left), rows(*right))
    high, low = split2(weights * signal_f)
    turned = transposed(writer)
    state[...] = state_now * jnp.exp(shrink) + dot(lanes(turned, turned), rows(high, low))


def statistics_kernel(
    table_ref, mine_ref, other_ref, local_ref, reader_ref, gating_ref, gain_ref, cotangent_ref,
    output_ref, statistics_ref,
):
    width = local_ref.shape[1]
    group = padded(width // HEAD_DIM)
    parity = lax.axis_index("context") % 2
    c = pl.program_id(0)
    blocks = pl.num_programs(0)
    reader = reader_ref[...]
    incoming = joined(mine_ref, other_ref, parity, reader.shape[1])
    high, low = split2(incoming)
    opening = dot(columns([jnp.exp(part(table_ref[...], ALL, group))]), spread(0, group, width))
    output = local_ref[...] + opening * dot(lanes(reader, reader), rows(high, low))
    output_ref[...] = output
    gating = gating_ref[...].astype(F32)
    gated = output * (gating / (1.0 + jnp.exp(-gating)))
    weighted = gain_ref[...] * cotangent_ref[...].astype(F32)
    ones = jnp.ones((8, 2 * width), BF16)
    squares = dot_nt(ones, lanes(*split2(gated * gated)))
    inner = dot_nt(ones, lanes(*split2(weighted * gated)))
    statistics_ref[pl.ds(c, 1), :] = squares[:1]
    statistics_ref[pl.ds(blocks + c, 1), :] = inner[:1]


def influence_kernel(
    full_width, table_ref, *refs
):
    statistics_refs = refs[:-10]
    (
        output_ref, reader_ref, gating_ref, gain_ref, cotangent_ref,
        grad_output_ref, grad_gating_ref, mine_ref, theirs_ref, state,
    ) = refs[-10:]
    width = output_ref.shape[1]
    group = padded(width // HEAD_DIM)
    parity = lax.axis_index("context") % 2
    c = pl.program_id(0)
    blocks = pl.num_programs(0)

    @pl.when(c == 0)
    def _():
        state[...] = jnp.zeros_like(state)

    squares = sum(ref[pl.ds(c, 1), :] for ref in statistics_refs)
    inner = sum(ref[pl.ds(blocks + c, 1), :] for ref in statistics_refs)
    scaling = lax.rsqrt(squares / full_width + EPSILON)
    pull = scaling * scaling * scaling * inner / full_width
    count = width // BLOCK
    scaling = lanes(*([jnp.broadcast_to(scaling, (BLOCK, BLOCK)).T] * count))
    pull = lanes(*([jnp.broadcast_to(pull, (BLOCK, BLOCK)).T] * count))
    output = output_ref[...]
    gating = gating_ref[...].astype(F32)
    sigmoid = 1.0 / (1.0 + jnp.exp(-gating))
    activation = gating * sigmoid
    weighted = gain_ref[...] * cotangent_ref[...].astype(F32)
    grad_gated = weighted * scaling - output * activation * pull
    grad_output = grad_gated * activation
    grad_output_ref[...] = grad_output
    grad_gating_ref[...] = (
        grad_gated * output * sigmoid * (1.0 + gating * (1.0 - sigmoid))
    ).astype(BF16)
    overall = part(table_ref[...], ALL, group)
    opening = dot(columns([jnp.exp(overall)]), spread(0, group, width))
    high, low = split2(opening * grad_output)
    turned = transposed(reader_ref[...])
    state[...] += dot(lanes(turned, turned), rows(high, low))

    @pl.when(c == blocks - 1)
    def _():
        total = jnp.broadcast_to(overall[:, BLOCK - 1 : BLOCK], (group, BLOCK))
        totals = lane_totals(total, group, width)[:8]
        mine, theirs = halves(rows(state[...], totals), parity)
        mine_ref[...] = mine
        theirs_ref[...] = theirs


def packed(x, core):
    half = BLOCK // 2
    top, bottom = x[:half], x[half:]
    low_lane = iota(top.shape, 1) < x.shape[1] // 2
    first = jnp.where(low_lane, top, pltpu.roll(bottom, x.shape[1] // 2, 1))
    second = jnp.where(low_lane, pltpu.roll(top, x.shape[1] // 2, 1), bottom)
    return jnp.where(core == 0, first, second), jnp.where(core == 0, second, first)


def backward_kernel(
    skip_ref, table_ref, mine_ref, other_ref, states_ref, signal_ref, writer_ref, reader_ref,
    output_ref, grad_output_ref,
    grad_signal_ref, grad_writer_ref, keep_ref, send_ref, sums_ref, state,
):
    width = signal_ref.shape[1]
    head_count = width // HEAD_DIM
    group = padded(head_count)
    parity = lax.axis_index("context") % 2

    @pl.when(pl.program_id(0) == 0)
    def _():
        state[...] = jnp.zeros_like(state)

    table = table_ref[...]
    run, late, step = part(table, RUN, group), part(table, LATE, group), part(table, DT, group)
    total = run[:, BLOCK - 1 : BLOCK]
    begun = part(table, ALL, group)[:, :1] - run[:, :1]
    signal, writer, reader = signal_ref[...], writer_ref[...], reader_ref[...]
    signal_f = signal.astype(F32)
    grad = grad_output_ref[...]
    cols = columns([jnp.exp(run), jnp.exp(total - run) * step])
    opening = dot(cols, spread(0, group, width))
    weights = dot(cols, spread(1, group, width))
    shrink = lane_totals(jnp.broadcast_to(total, (group, BLOCK)), group, width)
    start = lane_totals(jnp.broadcast_to(begun, (group, BLOCK)), group, width)
    incoming = joined(mine_ref, other_ref, parity, writer.shape[1])
    forward_state = states_ref[0] + jnp.exp(start) * incoming
    later = state[...]
    later_high, later_low = split2(later)
    skip = head_scalars(skip_ref, (1, width), 1, HEAD_DIM)
    flow = weights * dot(lanes(writer, writer), rows(later_high, later_low))
    scores = dot_nt(writer, reader)
    allowed = causal_mask(True)
    late_cols = plain_columns(late)
    low_lane = iota((BLOCK, BLOCK), 1) < HEAD_DIM
    grad_high, grad_low = split2(grad)
    grad_high_f, grad_low_f = grad_high.astype(F32), grad_low.astype(F32)
    grad_scores = jnp.zeros((BLOCK, BLOCK), F32)
    inside = []
    for j in range(head_count // 2):
        cut = slice(j * BLOCK, (j + 1) * BLOCK)
        pair = signal_f[:, cut]
        pieces = lanes(grad_high[:, cut], grad_low[:, cut])
        left, right = [], []
        for k in range(2):
            h = 2 * j + k
            ours = low_lane == (k == 0)
            gap = run[h : h + 1, :] - late_cols[:, h : h + 1]
            decay = jnp.exp(jnp.where(allowed, gap, NEGATIVE))
            high, low = split2(scores * decay)
            own_high = jnp.where(ours, grad_high_f[:, cut], 0.0).astype(BF16)
            own_low = jnp.where(ours, grad_low_f[:, cut], 0.0).astype(BF16)
            left += [high, low, high]
            right += [own_high, own_high, own_low]
            own = jnp.where(ours, pair, 0.0).astype(BF16)
            grad_scores = grad_scores + decay * dot_nt(lanes(own, own), pieces)
        inside.append(dot(lanes(*left), rows(*right)))
    through = lanes(*inside) + flow
    grad_signal = through + skip * grad
    grad_signal_ref[...] = grad_signal
    heads = gather_heads(group, width, 2)
    change = output_ref[...] * grad - signal_f * grad_signal
    sums_ref[...] = rows(
        dot_nt(heads, lanes(*split2(change))),
        dot_nt(heads, lanes(*split2(signal_f * through))),
    )
    opened = opening * grad
    opened_high, opened_low = split2(opened)
    state_high, state_low = split2(forward_state)
    high, low = split2(grad_scores)
    turned_high, turned_low = split2(grad_scores.T)
    grad_reader = dot(lanes(turned_high, turned_low), rows(writer, writer)) + dot_nt(
        lanes(opened_high, opened_low, opened_high), lanes(state_high, state_high, state_low)
    )
    weighed_high, weighed_low = split2(weights * signal_f)
    grad_writer_ref[...] = dot(lanes(high, low), rows(reader, reader)) + dot_nt(
        lanes(weighed_high, weighed_low, weighed_high), lanes(later_high, later_high, later_low)
    )
    keep, send = packed(grad_reader, lax.axis_index("dp") % 2)
    keep_ref[...] = keep
    send_ref[...] = send
    turned = transposed(reader)
    state[...] = later * jnp.exp(shrink) + dot(lanes(turned, turned), rows(opened_high, opened_low))


def closing_kernel(
    decay_ref, table_ref, end_mine_ref, end_other_ref, start_mine_ref, start_other_ref,
    later_mine_ref, later_other_ref, sums_ref, signal_ref, writer_ref,
    grad_signal_in_ref, grad_writer_ref,
    grad_signal_ref, grad_step_ref, keep_ref, send_ref, carry,
):
    width = signal_ref.shape[1]
    head_count = width // HEAD_DIM
    group = padded(head_count)
    parity = lax.axis_index("context") % 2
    table = table_ref[...]
    writer = writer_ref[...]
    count = writer.shape[1]
    later = joined(later_mine_ref, later_other_ref, parity, count)
    later_high, later_low = split2(later)
    heads = gather_heads(group, width, 2)

    @pl.when(pl.program_id(0) == 0)
    def _():
        end = joined(end_mine_ref, end_other_ref, parity, count + 8)
        start = joined(start_mine_ref, start_other_ref, parity, count)
        final = end[:count] + jnp.exp(end[count : count + 1]) * start
        crossing = jnp.sum(final * later, axis=0, keepdims=True)
        carry[...] = dot_nt(heads, lanes(*split2(jnp.broadcast_to(crossing, (BLOCK, width)))))

    signal_f = signal_ref[...].astype(F32)
    last = part(table, LAST, group)
    weights = dot(columns([last]), spread(0, group, width))
    flow = weights * dot(lanes(writer, writer), rows(later_high, later_low))
    grad_signal_ref[...] = (grad_signal_in_ref[...] + flow).astype(BF16)
    weighed_high, weighed_low = split2(weights * signal_f)
    grad_writer = grad_writer_ref[...] + dot_nt(
        lanes(weighed_high, weighed_low, weighed_high), lanes(later_high, later_high, later_low)
    )
    keep, send = packed(grad_writer, lax.axis_index("dp") % 2)
    keep_ref[...] = keep
    send_ref[...] = send
    added = dot_nt(heads, lanes(*split2(signal_f * flow)))
    sums = sums_ref[...]
    change = sums[:group] - added
    lower = causal_mask(False).astype(F32).astype(BF16)
    crossing = sum(dot(p, lower) for p in split3(change)) + carry[...]
    carry[...] = jnp.broadcast_to(crossing[:, :1], (group, BLOCK))
    rate = -jnp.exp(head_scalars(decay_ref, (group, BLOCK), 0, 1))
    grad_step = (sums[group:] + added) / part(table, DT, group) + rate * crossing
    turned = plain_columns(grad_step * part(table, SIG, group))
    grad_step_ref[...] = turned[:, :head_count]


def sum_kernel(writer_ref, writer_got_ref, reader_ref, reader_got_ref, out_ref):
    dp = lax.axis_index("dp")
    total = jnp.where(
        dp < 2, writer_ref[...] + writer_got_ref[...], reader_ref[...] + reader_got_ref[...]
    )
    half = total.shape[1] // 2
    for c in range(total.shape[0] // (BLOCK // 2)):
        piece = total[c * (BLOCK // 2) : (c + 1) * (BLOCK // 2)]
        out_ref[c * BLOCK : c * BLOCK + BLOCK // 2, :] = piece[:, :half]
        out_ref[c * BLOCK + BLOCK // 2 : (c + 1) * BLOCK, :] = piece[:, half:]


def combine(earlier, later, count):
    total = later[count : count + 1, :]
    state_row = jnp.arange(earlier.shape[0])[:, None] < count
    return jnp.where(state_row, earlier * jnp.exp(total), earlier) + later


def exchange(mine, theirs, devices, backwards):
    count = mine.shape[0] - 8
    place = lax.axis_index("context") % 2
    first = place == (1 if backwards else 0)
    partner = [(i, i ^ 1) for i in range(devices)]
    other = lax.ppermute(theirs, "context", partner)
    one = jnp.where(first, mine, other)
    two = jnp.where(first, other, mine)
    window = combine(one, two, count)
    before = None
    distance = 1
    while 2 * distance < devices:
        pairs = [(i, i + 2 * distance) for i in range(devices - 2 * distance)]
        if backwards:
            pairs = [(b, a) for a, b in pairs]
        got = lax.ppermute(window, "context", pairs)
        before = got if before is None else combine(got, before, count)
        if 4 * distance < devices:
            window = combine(got, window, count)
        distance *= 2
    if before is None:
        before = jnp.zeros_like(mine)
    after = combine(before, one, count)
    received = lax.ppermute(jnp.where(first, after, before), "context", partner)
    return jnp.where(first, before, after), received


def on_device(
    dp_size, context_size,
    signal, gating, writer, reader, step_raw, decay_log, skip_gain, norm_gain, cotangent,
):
    tokens, width = signal.shape
    count = writer.shape[1]
    head_count = step_raw.shape[1]
    group = padded(head_count)
    blocks = tokens // BLOCK
    full_width = width * dp_size
    gain = norm_gain[None, :]
    smem = pl.BlockSpec(memory_space=pltpu.SMEM)
    shape = jax.ShapeDtypeStruct
    half_state = shape((count + 8, width // 2), F32)
    wide = (BLOCK, width)
    narrow = (BLOCK, count)

    def ahead(block):
        return pl.BlockSpec(block, lambda c: (c, 0))

    def behind(block):
        return pl.BlockSpec(block, lambda c: (blocks - 1 - c, 0))

    def whole(s):
        return pl.BlockSpec(s, lambda c: (0,) * len(s))

    half_spec = whole(half_state.shape)
    table_ahead = pl.BlockSpec((6 * group, BLOCK), lambda c: (0, c))
    table_behind = pl.BlockSpec((6 * group, BLOCK), lambda c: (0, blocks - 1 - c))

    vmem = pl.BlockSpec(memory_space=pltpu.VMEM)
    table, end_mine, end_theirs = pl.pallas_call(
        ends_kernel,
        in_specs=[smem, vmem, vmem, vmem],
        out_specs=[vmem, vmem, vmem],
        out_shape=[shape((6 * group, tokens), F32), half_state, half_state],
        name="ends",
    )(decay_log, step_raw, signal, writer)

    start_mine, start_other = exchange(end_mine, end_theirs, context_size, False)

    local, states = pl.pallas_call(
        forward_kernel,
        grid=(blocks,),
        in_specs=[smem, table_ahead, ahead(wide), ahead(narrow), ahead(narrow)],
        out_specs=[ahead(wide), pl.BlockSpec((1, count, width), lambda c: (c, 0, 0))],
        out_shape=[shape((tokens, width), F32), shape((blocks, count, width), F32)],
        scratch_shapes=[pltpu.VMEM((count, width), F32)],
        name="forward",
    )(skip_gain, table, signal, writer, reader)

    output, statistics = pl.pallas_call(
        statistics_kernel,
        grid=(blocks,),
        in_specs=[
            table_ahead, half_spec, half_spec, ahead(wide), ahead(narrow), ahead(wide),
            whole((1, width)), ahead(wide),
        ],
        out_specs=[ahead(wide), whole((2 * blocks, BLOCK))],
        out_shape=[shape((tokens, width), F32), shape((2 * blocks, BLOCK), F32)],
        name="statistics",
    )(table, start_mine, start_other, local, reader, gating, gain, cotangent)

    if dp_size <= 4:
        shares = [statistics] + [
            lax.ppermute(statistics, "dp", [(i, i ^ k) for i in range(dp_size)])
            for k in range(1, dp_size)
        ]
    else:
        shares = [lax.psum(statistics, "dp")]

    grad_output, grad_gating, mine, theirs = pl.pallas_call(
        partial(influence_kernel, full_width),
        grid=(blocks,),
        in_specs=[table_ahead]
        + [whole((2 * blocks, BLOCK))] * len(shares)
        + [ahead(wide), ahead(narrow), ahead(wide), whole((1, width)), ahead(wide)],
        out_specs=[ahead(wide), ahead(wide), half_spec, half_spec],
        out_shape=[shape((tokens, width), F32), shape((tokens, width), BF16), half_state, half_state],
        scratch_shapes=[pltpu.VMEM((count, width), F32)],
        name="influence",
    )(table, *shares, output, reader, gating, gain, cotangent)

    later_mine, later_other = exchange(mine, theirs, context_size, True)

    pack = (BLOCK // 2, count)
    pack_shape = shape((tokens // 2, count), F32)
    grad_local, writer_local, reader_keep, reader_send, sums = pl.pallas_call(
        backward_kernel,
        grid=(blocks,),
        in_specs=[
            smem, table_behind, half_spec, half_spec,
            pl.BlockSpec((1, count, width), lambda c: (blocks - 1 - c, 0, 0)),
            behind(wide), behind(narrow), behind(narrow), behind(wide), behind(wide),
        ],
        out_specs=[
            behind(wide), behind(narrow), behind(pack), behind(pack),
            pl.BlockSpec((2 * group, BLOCK), lambda c: (0, blocks - 1 - c)),
        ],
        out_shape=[
            shape((tokens, width), F32), shape((tokens, count), F32), pack_shape, pack_shape,
            shape((2 * group, tokens), F32),
        ],
        scratch_shapes=[pltpu.VMEM((count, width), F32)],
        name="backward",
    )(skip_gain, table, start_mine, start_other, states, signal, writer, reader, output, grad_output)

    grad_signal, grad_step, writer_keep, writer_send = pl.pallas_call(
        closing_kernel,
        grid=(blocks,),
        in_specs=[smem, table_behind]
        + [half_spec] * 6
        + [
            pl.BlockSpec((2 * group, BLOCK), lambda c: (0, blocks - 1 - c)),
            behind(wide), behind(narrow), behind(wide), behind(narrow),
        ],
        out_specs=[behind(wide), behind((BLOCK, head_count)), behind(pack), behind(pack)],
        out_shape=[
            shape((tokens, width), BF16), shape((tokens, head_count), F32), pack_shape, pack_shape,
        ],
        scratch_shapes=[pltpu.VMEM((group, BLOCK), F32)],
        name="closing",
    )(
        decay_log, table, end_mine, end_theirs, start_mine, start_other, later_mine, later_other,
        sums, signal, writer, grad_local, writer_local,
    )

    cores = [(i, i ^ 1) for i in range(dp_size)]
    reader_part = reader_keep + lax.ppermute(reader_send, "dp", cores)
    writer_part = writer_keep + lax.ppermute(writer_send, "dp", cores)
    if dp_size == 4:
        reader_got = lax.ppermute(reader_part, "dp", [(0, 2), (1, 3)])
        writer_got = lax.ppermute(writer_part, "dp", [(2, 0), (3, 1)])
        grad_bc = pl.pallas_call(
            sum_kernel,
            in_specs=[vmem] * 4,
            out_specs=vmem,
            out_shape=shape((tokens, count // 2), F32),
            name="total",
        )(writer_part, writer_got, reader_part, reader_got)
    else:
        half = count // 2
        place = lax.axis_index("dp") % 2

        def unpacked(x):
            x = x.reshape(blocks, BLOCK // 2, 2, half).swapaxes(1, 2).reshape(tokens, half)
            zero = jnp.zeros_like(x)
            return jnp.where(place == 0, lanes(x, zero), lanes(zero, x))

        both = lanes(unpacked(writer_part), unpacked(reader_part))
        grad_bc = lax.psum_scatter(both, "dp", scatter_dimension=1, tiled=True)
    return grad_signal, grad_gating, grad_bc, grad_step


def solution(mesh):
    sharded = P("context", "dp")
    shared = P("context", None)
    in_specs = (
        sharded, sharded, shared, shared, sharded, P("dp"), P("dp"), P("dp"), sharded,
    )
    return jax.shard_map(
        partial(on_device, mesh.shape["dp"], mesh.shape["context"]),
        mesh=mesh, in_specs=in_specs, out_specs=(sharded,) * 4, check_vma=False,
    )
```
